32 devices in a mesh: gx: 8 (over z, y), gy: 4 (over x, core).
Axes of the slice: x: 2, y: 2, z: 4, core: 2. Of those that a mesh axis runs over, the one named last changes fastest.
Arguments:
- conc: float32 [32, 64, 1024], P('gx', 'gy'), may hold values from -2 to 2
- order: float32 [3, 32, 64, 1024], P(None, 'gx', 'gy'), may hold values from -1.5 to 1.5
Outputs:
- displacement: float32 [3, 32, 64, 1024], P(None, 'gx', 'gy')
- conc_new: float32 [32, 64, 1024], P('gx', 'gy')
- order_new: float32 [3, 32, 64, 1024], P(None, 'gx', 'gy')
The draws below stay inside these ranges and needn't reach their ends.
All inputs are finite; a program needn't handle non-finite values.
Results may differ from the reference program's by a relative error of at most 0.0001.
Values sent between devices are 32-bit elements; how exact they have to be, the bound alone decides.
A program may use at most 64 MiB of HBM per device.

```python
import math
import jax
import jax.numpy as jnp

CZ = 1024
ITERS = 3
NX = 32
NY = 64


def rough_field(key, leading, trend_low, trend_high, rough_low, rough_high, cross_low, cross_high, amplitude):
    keys = jax.random.split(key, 4)
    position = jnp.arange(NX, dtype=jnp.float32) / NX
    trend = trend_low + (trend_high - trend_low) * position
    rough = jnp.exp(jax.random.uniform(keys[0], (NX,), jnp.float32, math.log(rough_low), math.log(rough_high)))
    cross = jnp.exp(jax.random.uniform(keys[1], (NY,), jnp.float32, math.log(cross_low), math.log(cross_high)))
    ramp = jnp.arange(NY, dtype=jnp.float32) / max(NY - 1, 1)
    rough_weight = 0.15 + 0.85 * ramp
    smooth_weight = 1.0 - ramp
    base = jax.random.uniform(keys[2], (leading, NX, NY, CZ), jnp.float32, -1.0, 1.0)
    phases = jax.random.uniform(keys[3], (2, leading), jnp.float32, 0.0, 1.0)
    wave_x = max(1, NX // 32)
    wave_z = max(1, CZ // 32)
    depth = jnp.arange(CZ, dtype=jnp.float32) / CZ
    along_x = jnp.cos(2.0 * math.pi * (wave_x * position[None, :] + phases[0][:, None]))
    along_z = jnp.cos(2.0 * math.pi * (wave_z * depth[None, :] + phases[1][:, None]))
    smooth = along_x[:, :, None, None] * along_z[:, None, None, :]
    scale = (trend * rough)[None, :, None, None] * (cross * rough_weight)[None, None, :, None]
    return amplitude * (scale * base + 0.9 * smooth_weight[None, None, :, None] * smooth)


def draw_conc(key, part):
    field = rough_field(jax.random.fold_in(key, 3), 1, 0.45, 1.35, 0.8, 1.25, 0.8, 1.0, 1.0)
    return field[0]


def draw_order(key, part):
    field = rough_field(jax.random.fold_in(key, 5), 3, 0.45, 1.35, 0.8, 1.25, 0.8, 1.0, 0.75)
    return field


def setup_inputs(seed: int = 0) -> dict:
    arg_keys = jax.random.split(jax.random.key(seed), 3)
    return {
        "conc": draw_conc(jax.random.fold_in(arg_keys[2], 71), 0),
        "order": draw_order(jax.random.fold_in(arg_keys[2], 71), 0),
    }


LAME_LAMBDA = 1.0
SHEAR_MODULUS = 1.0
VEGARD_STRAIN = 1.0
TETRA_STRAIN = 2.0
AXIAL_STRAIN = -0.5
COUPLING = 0.5
WELL_DEPTH = 1.0
GRADIENT_CONC = 0.5
GRADIENT_ORDER = 0.5
TIME_STEP = 0.02
MOBILITY = 1.0
RELAXATION = 1.0


def coefficient(variant, axis):
    return TETRA_STRAIN if variant == axis else AXIAL_STRAIN


def periodic_laplace(field):
    result = -6.0 * field
    for axis in (-3, -2, -1):
        result = result + jnp.roll(field, 1, axis) + jnp.roll(field, -1, axis)
    return result


def periodic_central(field, axis):
    return 0.5 * (jnp.roll(field, -1, axis) - jnp.roll(field, 1, axis))


def eigen_stress(conc, order):
    misfit = []
    for axis in range(3):
        value = VEGARD_STRAIN * conc
        for variant in range(3):
            value = value + order[variant] * order[variant] * coefficient(variant, axis)
        misfit.append(value)
    trace = misfit[0] + misfit[1] + misfit[2]
    return misfit, [LAME_LAMBDA * trace + 2.0 * SHEAR_MODULUS * item for item in misfit]


def stencil(padded):
    offsets = [(1, 0, 0), (0, 1, 0), (0, 0, 1)]

    def pick(comp, shift_x, shift_y, shift_z):
        return padded[comp, 1 + shift_x:padded.shape[1] - 1 + shift_x, 1 + shift_y:padded.shape[2] - 1 + shift_y, 1 + shift_z:padded.shape[3] - 1 + shift_z]

    def plus(first, second, sign):
        return tuple(first[k] + sign * second[k] for k in range(3))

    zero = (0, 0, 0)
    result = []
    for i in range(3):
        center = pick(i, 0, 0, 0)
        laplace = -6.0 * center
        for axis in range(3):
            laplace = laplace + pick(i, *offsets[axis]) + pick(i, *plus(zero, offsets[axis], -1))
        graddiv = pick(i, *offsets[i]) + pick(i, *plus(zero, offsets[i], -1)) - 2.0 * center
        for j in range(3):
            if j != i:
                both = plus(offsets[i], offsets[j], 1)
                cross = plus(offsets[i], offsets[j], -1)
                graddiv = graddiv + 0.25 * (pick(j, *both) - pick(j, *cross) - pick(j, *plus(zero, cross, -1)) + pick(j, *plus(zero, both, -1)))
        result.append(-SHEAR_MODULUS * laplace - (LAME_LAMBDA + SHEAR_MODULUS) * graddiv)
    return jnp.stack(result)


def normal_strain(padded):
    strain_x = 0.5 * (padded[0, 2:, 1:-1, 1:-1] - padded[0, :-2, 1:-1, 1:-1])
    strain_y = 0.5 * (padded[1, 1:-1, 2:, 1:-1] - padded[1, 1:-1, :-2, 1:-1])
    strain_z = 0.5 * (padded[2, 1:-1, 1:-1, 2:] - padded[2, 1:-1, 1:-1, :-2])
    return [strain_x, strain_y, strain_z]


def stiffness(field):
    return stencil(jnp.pad(field, ((0, 0), (1, 1), (1, 1), (1, 1))))


def reference(conc, order):
    misfit, eigen = eigen_stress(conc, order)
    rhs = jnp.stack([-periodic_central(eigen[axis], axis) for axis in range(3)])
    displacement = jnp.zeros_like(rhs)
    residual = rhs
    direction = rhs
    norm_now = jnp.sum(residual * residual)
    for step in range(ITERS):
        image = stiffness(direction)
        alpha = norm_now / jnp.sum(direction * image)
        displacement = displacement + alpha * direction
        residual = residual - alpha * image
        norm_next = jnp.sum(residual * residual)
        direction = residual + (norm_next / norm_now) * direction
        norm_now = norm_next
    strain = normal_strain(jnp.pad(displacement, ((0, 0), (1, 1), (1, 1), (1, 1))))
    strain_trace = strain[0] + strain[1] + strain[2]
    misfit_trace = misfit[0] + misfit[1] + misfit[2]
    stress = [LAME_LAMBDA * (strain_trace - misfit_trace) + 2.0 * SHEAR_MODULUS * (strain[a] - misfit[a]) for a in range(3)]
    total = order[0] * order[0] + order[1] * order[1] + order[2] * order[2]
    potential = conc * conc * conc - conc - COUPLING * total - GRADIENT_CONC * periodic_laplace(conc)
    conc_new = conc + TIME_STEP * MOBILITY * periodic_laplace(potential)
    drives = []
    for variant in range(3):
        elastic = stress[0] * coefficient(variant, 0) + stress[1] * coefficient(variant, 1) + stress[2] * coefficient(variant, 2)
        drive = (total - WELL_DEPTH - 2.0 * COUPLING * conc) * order[variant] - GRADIENT_ORDER * periodic_laplace(order[variant]) - 2.0 * order[variant] * elastic
        drives.append(drive)
    order_new = order - TIME_STEP * RELAXATION * jnp.stack(drives)
    return displacement, conc_new, order_new
```

```python
import functools

import jax
import jax.numpy as jnp
from jax import lax
from jax.experimental import pallas as pl
from jax.experimental.pallas import tpu as pltpu
from jax.sharding import PartitionSpec as P

MESH = pl.DeviceIdType.MESH
LANES = 128
DIRS = [(dx, dy) for dx in (-1, 0, 1) for dy in (-1, 0, 1) if (dx, dy) != (0, 0)]
SIDES = [(-1, 0), (1, 0), (0, -1), (0, 1)]
TIME_STEP = 0.02
DIAGONAL = 10.0


def kernel(nx, ny, X, Y, S, conc_hbm, order_hbm, disp_hbm, cnew_hbm, onew_hbm,
           nat, xh, ph, v, pot, base, od, oc, gat,
           lsem, osem, a_send, a_recv, v_send, v_recv, p_send, p_recv, g_send, g_recv):
    gx = lax.axis_index("gx")
    gy = lax.axis_index("gy")
    N = nx * ny
    me = gx * ny + gy
    lane = lax.broadcasted_iota(jnp.int32, (S, LANES), 1)
    sub = lax.broadcasted_iota(jnp.int32, (S, LANES), 0)
    last_lane = lane == LANES - 1
    first_lane = lane == 0
    z_end = jnp.logical_and(last_lane, sub == S - 1)
    z_start = jnp.logical_and(first_lane, sub == 0)
    zero = jnp.zeros((S, LANES), jnp.float32)

    loads = [
        pltpu.make_async_copy(conc_hbm, nat.at[0], lsem.at[0]),
        pltpu.make_async_copy(order_hbm, nat.at[pl.ds(1, 3)], lsem.at[1]),
    ]
    for item in loads:
        item.start()

    barrier = pltpu.get_barrier_semaphore()

    def greet(j, carry):
        t = lax.rem(me + j, N)
        pl.semaphore_signal(barrier, inc=1, device_id=(t // ny, lax.rem(t, ny)), device_id_type=MESH)
        return carry

    lax.fori_loop(1, N, greet, 0)
    pl.semaphore_wait(barrier, N - 1)

    def device(dx, dy):
        return (lax.rem(gx + dx + nx, nx), lax.rem(gy + dy + ny, ny))

    def remote(src, dst, send, recv, d):
        return pltpu.make_async_remote_copy(
            src_ref=src, dst_ref=dst, send_sem=send, recv_sem=recv,
            device_id=device(*d), device_id_type=MESH)

    def cell(y):
        return pl.ds(pl.multiple_of(y * S, S), S)

    def own(count, extent, step):
        if step == 0:
            return (pl.ds(1, extent), pl.ds(1, extent))
        return (pl.ds(1, 1), pl.ds(extent + 1, 1)) if step < 0 else (pl.ds(extent, 1), pl.ds(0, 1))

    def rows(part):
        return pl.ds(part.start * S, part.size * S)

    a_copies = []
    for n, (dx, face, side) in enumerate(((-1, 0, 1), (1, X - 1, 0))):
        a_copies.append(remote(conc_hbm.at[face], xh.at[side, 0], a_send.at[2 * n], a_recv.at[2 * n], (dx, 0)))
        a_copies.append(remote(order_hbm.at[:, face], xh.at[side, pl.ds(1, 3)], a_send.at[2 * n + 1],
                               a_recv.at[2 * n + 1], (dx, 0)))
    for item in a_copies:
        item.start()
    for item in loads:
        item.wait()

    def to_cells(read, f, x):
        for y0 in range(0, Y, 8):
            for c in range(S):
                ph[f, x, pl.ds((1 + y0) * S + c, 8, stride=S), :] = read(y0, c)

    def relayout(i, carry):
        f, x = i // X, lax.rem(i, X)
        to_cells(lambda y0, c: nat[f, x, pl.ds(y0, 8), pl.ds(c * LANES, LANES)], f, x + 1)
        return carry

    lax.fori_loop(0, 4 * X, relayout, 0)
    y_copies = []
    for n, dy in enumerate((-1, 1)):
        src, dst = own(ny, Y, dy)
        y_copies.append(remote(ph.at[:, pl.ds(1, X), rows(src)], ph.at[:, pl.ds(1, X), rows(dst)],
                               a_send.at[4 + n], a_recv.at[4 + n], (0, dy)))
    for item in y_copies:
        item.start()
    for item in a_copies:
        item.wait()

    def relayout_x(f, carry):
        for side in range(2):
            to_cells(lambda y0, c: xh[side, f, pl.ds(y0, 8), pl.ds(c * LANES, LANES)], f, side * (X + 1))
        return carry

    lax.fori_loop(0, 4, relayout_x, 0)
    for item in y_copies:
        item.wait()

    def up(a):
        r = pltpu.roll(a, LANES - 1, 1)
        return jnp.where(last_lane, pltpu.roll(r, S - 1, 0), r)

    def down(a):
        r = pltpu.roll(a, 1, 1)
        return jnp.where(first_lane, pltpu.roll(r, 1, 0), r)

    def up0(a):
        return jnp.where(z_end, 0.0, up(a))

    def down0(a):
        return jnp.where(z_start, 0.0, down(a))

    def cells(body, init=0):
        def outer(y, carry):
            for x in range(1, X + 1):
                carry = body(x, y, carry)
            return carry
        return lax.fori_loop(1, Y + 1, outer, init)

    def rhs(x, y, carry):
        def load(f, xx, yy):
            return ph[f, xx, cell(yy), :]

        def eig(a, xx, yy):
            o = load(1 + a, xx, yy)
            return load(0, xx, yy) + o * o
        r0 = -2.5 * (eig(0, x + 1, y) - eig(0, x - 1, y))
        r1 = -2.5 * (eig(1, x, y + 1) - eig(1, x, y - 1))
        e = eig(2, x, y)
        r2 = -2.5 * (up(e) - down(e))
        v[0, 0, x, cell(y), :] = r0
        v[0, 1, x, cell(y), :] = r1
        v[0, 2, x, cell(y), :] = r2
        return carry + (r0 * r0 + r1 * r1 + r2 * r2)

    acc0 = cells(rhs, zero)

    def valid(dx, dy):
        ok = None
        for g, n, d in ((gx, nx, dx), (gy, ny, dy)):
            if d:
                t = g > 0 if d < 0 else g < n - 1
                ok = t if ok is None else jnp.logical_and(ok, t)
        return ok

    def v_copy(k, n):
        dx, dy = DIRS[n]
        sx, tx = own(nx, X, dx)
        sy, ty = own(ny, Y, dy)
        comps = pl.ds(0, 2) if dx and dy else pl.ds(0, 3)
        return remote(v.at[k, comps, sx, rows(sy)], v.at[k, comps, tx, rows(ty)],
                      v_send.at[k, n], v_recv.at[k, n], (dx, dy))

    def v_start(k):
        for n in sorted(range(8), key=lambda n: (DIRS[n][0] == 0, DIRS[n][1] != 0)):
            @pl.when(valid(*DIRS[n]))
            def _():
                v_copy(k, n).start()

    def v_wait(k):
        for n, (dx, dy) in enumerate(DIRS):
            @pl.when(valid(dx, dy))
            def _():
                v_copy(k, n).wait_send()

            @pl.when(valid(-dx, -dy))
            def _():
                v_copy(k, n).wait_recv()

    v_start(0)

    def clear_x(row):
        def body(i, carry):
            for k in range(3):
                for a in range(3):
                    v[k, a, row, cell(i), :] = zero
            return carry
        lax.fori_loop(0, Y + 2, body, 0)

    def clear_y(col, low, high):
        for k in range(3):
            for a in range(3):
                for x in range(low, high):
                    v[k, a, x, cell(col), :] = zero

    for cond, row in ((gx == 0, 0), (gx == nx - 1, X + 1)):
        @pl.when(cond)
        def _(row=row):
            clear_x(row)
    for cond, col in ((gy == 0, 0), (gy == ny - 1, Y + 1)):
        @pl.when(cond)
        def _(col=col):
            clear_y(col, 0, X + 2)

    def laplace(read, x, y):
        c = read(x, y)
        s = read(x + 1, y) + read(x - 1, y) + read(x, y + 1) + read(x, y - 1)
        return s + up(c) + down(c) - 6.0 * c

    def potential(x, y, carry):
        c = ph[0, x, cell(y), :]
        o = [ph[1 + p, x, cell(y), :] for p in range(3)]
        total = o[0] * o[0] + o[1] * o[1] + o[2] * o[2]
        lap = laplace(lambda xx, yy: ph[0, xx, cell(yy), :], x, y)
        pot[x, cell(y), :] = c * c * c - c - 0.5 * total - 0.5 * lap
        return carry

    cells(potential)
    p_copies = []
    for n, (dx, dy) in enumerate(SIDES):
        sx, tx = own(nx, X, dx)
        sy, ty = own(ny, Y, dy)
        p_copies.append(remote(pot.at[sx, rows(sy)], pot.at[tx, rows(ty)], p_send.at[n], p_recv.at[n], (dx, dy)))
    for item in p_copies:
        item.start()

    def stencil(k, x, y):
        def u(a, dx, dy):
            return v[k, a, x + dx, cell(y + dy), :]
        cross = []
        for a in (0, 1):
            cross.append(0.5 * (u(a, 1, 1) - u(a, 1, -1) - u(a, -1, 1) + u(a, -1, -1)))
        xp = [u(a, 1, 0) for a in range(3)]
        xm = [u(a, -1, 0) for a in range(3)]
        yp = [u(a, 0, 1) for a in range(3)]
        ym = [u(a, 0, -1) for a in range(3)]
        c = [u(a, 0, 0) for a in range(3)]
        g = 0.5 * (xp[2] - xm[2])
        h = 0.5 * (yp[2] - ym[2])
        w = 0.5 * ((xp[0] - xm[0]) + (yp[1] - ym[1]))
        i0 = 3.0 * (xp[0] + xm[0]) + (yp[0] + ym[0]) + cross[1] + up0(c[0] + g) + down0(c[0] - g)
        i1 = (xp[1] + xm[1]) + 3.0 * (yp[1] + ym[1]) + cross[0] + up0(c[1] + h) + down0(c[1] - h)
        c3 = 3.0 * c[2]
        i2 = (xp[2] + xm[2]) + (yp[2] + ym[2]) + up0(c3 + w) + down0(c3 - w)
        return c, [i0, i1, i2]

    scale = -1.0 / DIAGONAL

    def first(x, y, carry):
        d01, d11 = carry
        c, image = stencil(0, x, y)
        for a in range(3):
            new = scale * image[a]
            v[1, a, x, cell(y), :] = new
            d01 = d01 + c[a] * new
            d11 = d11 + new * new
        return d01, d11

    v_wait(0)
    acc1 = cells(first, (zero, zero))
    v_start(1)

    def local(x, y, carry):
        c = ph[0, x, cell(y), :]
        o = [ph[1 + p, x, cell(y), :] for p in range(3)]
        q = [item * item for item in o]
        total = q[0] + q[1] + q[2]
        common = total - 1.0 - c
        for p in range(3):
            lap = laplace(lambda xx, yy: ph[1 + p, xx, cell(yy), :], x, y)
            misfit = c + 2.5 * q[p] - 0.5 * total
            trace = 3.0 * c + total
            elastic = 2.5 * (-trace - 2.0 * misfit) + 2.5 * trace
            drive = common * o[p] - 0.5 * lap - 2.0 * o[p] * elastic
            base[p, x - 1, cell(y - 1), :] = o[p] - TIME_STEP * drive
        return carry

    cells(local)

    def second(x, y, carry):
        d12, d22 = carry
        c, image = stencil(1, x, y)
        for a in range(3):
            new = (2.0 * scale) * image[a] - v[0, a, x, cell(y), :]
            v[2, a, x, cell(y), :] = new
            d12 = d12 + c[a] * new
            d22 = d22 + new * new
        return d12, d22

    v_wait(1)
    acc2 = cells(second, (zero, zero))
    v_start(2)

    for item in p_copies:
        item.wait()

    def conc_step(x, y, carry):
        lap = laplace(lambda xx, yy: pot[xx, cell(yy), :], x, y)
        pot_new = ph[0, x, cell(y), :] + TIME_STEP * lap
        oc[x - 1, cell(y - 1), :] = pot_new
        return carry

    cells(conc_step)

    def from_cells(read, f, x):
        for y0 in range(0, Y, 8):
            for c in range(S):
                nat[f, x, pl.ds(y0, 8), pl.ds(c * LANES, LANES)] = read(pl.ds(y0 * S + c, 8, stride=S))

    def conc_out(x, carry):
        from_cells(lambda r: oc[x, r, :], 0, x)
        return carry

    lax.fori_loop(0, X, conc_out, 0)
    c_store = pltpu.make_async_copy(nat.at[0], cnew_hbm, osem.at[0])
    c_store.start()

    def third(x, y, carry):
        c, image = stencil(2, x, y)
        return carry + (c[0] * image[0] + c[1] * image[1] + c[2] * image[2])

    v_wait(2)
    acc3 = scale * cells(third, zero)

    row_lane = lax.broadcasted_iota(jnp.int32, (1, LANES), 1)

    def reduce_all(a):
        return jnp.sum(jnp.sum(a, axis=0, keepdims=True), axis=1, keepdims=True)

    packed = jnp.zeros((1, LANES), jnp.float32)
    for n, item in enumerate((acc0, acc1[0], acc1[1], acc2[0], acc2[1], acc3)):
        packed = jnp.where(row_lane == n, reduce_all(item), packed)
    gat[me] = packed

    def g_copy(j, slot):
        t = lax.rem(me + j, N)
        return pltpu.make_async_remote_copy(
            src_ref=gat.at[slot], dst_ref=gat.at[slot], send_sem=g_send.at[j], recv_sem=g_recv.at[j],
            device_id=(t // ny, lax.rem(t, ny)), device_id_type=MESH)

    def g_start(j, carry):
        g_copy(j, me).start()
        return carry

    def g_wait(j, carry):
        g_copy(j, me).wait_send()
        g_copy(j, lax.rem(me + N - j, N)).wait_recv()
        return carry

    lax.fori_loop(1, N, g_start, 0)
    lax.fori_loop(1, N, g_wait, 0)
    tot = gat[0]
    for j in range(1, N):
        tot = tot + gat[j]
    m0, m1, d11, d12, d22, e = [
        jnp.sum(jnp.where(row_lane == n, tot, 0.0), axis=1, keepdims=True) for n in range(6)]

    g02 = 2.0 * d11 - m0
    G = [[m0, m1, g02], [m1, d11, d12], [g02, d12, d22]]
    h11 = 0.5 * (d12 + m1)
    h12 = 0.5 * (d22 + g02)
    H = [[m1, d11, d12], [d11, h11, h12], [d12, h12, e]]

    def form(mat, a, b):
        out = None
        for i in range(3):
            for j in range(3):
                if a[i] is not None and b[j] is not None:
                    term = a[i] * b[j] * mat[i][j]
                    out = term if out is None else out + term
        return out

    def plus(a, b):
        return b if a is None else (a if b is None else a + b)

    def times(s, a):
        return None if a is None else s * a

    A = [[DIAGONAL * (H[i][j] + G[i][j]) for j in range(3)] for i in range(3)]
    one = jnp.ones((1, 1), jnp.float32)
    xs, rs, ps = [None] * 3, [one, None, None], [one, None, None]
    rr = m0
    for it in range(3):
        alpha = rr / form(A, ps, ps)
        xs = [plus(xs[i], times(alpha, ps[i])) for i in range(3)]
        if it < 2:
            t = list(ps)
            t[1] = plus(t[1], ps[0])
            if ps[1] is not None:
                t[0] = plus(t[0], 0.5 * ps[1])
                t[2] = plus(t[2], 0.5 * ps[1])
            rs = [plus(rs[i], times(-DIAGONAL * alpha, t[i])) for i in range(3)]
            new = form(G, rs, rs)
            ps = [plus(rs[i], times(new / rr, ps[i])) for i in range(3)]
            rr = new
    co = [jnp.broadcast_to(item, (S, LANES)) for item in xs]

    def mix(a, x, y):
        return (co[0] * v[0, a, x, cell(y), :] + co[1] * v[1, a, x, cell(y), :]
                + co[2] * v[2, a, x, cell(y), :])

    def combine(x, y, carry):
        for a in range(3):
            od[a, x, cell(y), :] = mix(a, x, y)
        return carry

    cells(combine)

    def halo_x(y, carry):
        for x in (0, X + 1):
            od[0, x, cell(y), :] = mix(0, x, y)
        return carry

    lax.fori_loop(1, Y + 1, halo_x, 0)
    for x in range(1, X + 1):
        for y in (0, Y + 1):
            od[1, x, cell(y), :] = mix(1, x, y)

    c_store.wait()

    def disp_out(i, carry):
        a, x = i // X, lax.rem(i, X)
        for y0 in range(0, Y, 8):
            for c in range(S):
                nat[a, x, pl.ds(y0, 8), pl.ds(c * LANES, LANES)] = od[
                    a, x + 1, pl.ds((1 + y0) * S + c, 8, stride=S), :]
        return carry

    lax.fori_loop(0, 3 * X, disp_out, 0)
    d_store = pltpu.make_async_copy(nat.at[pl.ds(0, 3)], disp_hbm, osem.at[1])
    d_store.start()

    def final(x, y, carry):
        d2 = od[2, x, cell(y), :]
        strain = [
            0.5 * (od[0, x + 1, cell(y), :] - od[0, x - 1, cell(y), :]),
            0.5 * (od[1, x, cell(y + 1), :] - od[1, x, cell(y - 1), :]),
            0.5 * (up0(d2) - down0(d2)),
        ]
        trace = strain[0] + strain[1] + strain[2]
        for p in range(3):
            elastic = 2.5 * (trace + 2.0 * strain[p]) - 2.5 * trace
            base[p, x - 1, cell(y - 1), :] = (
                base[p, x - 1, cell(y - 1), :] + (2.0 * TIME_STEP) * ph[1 + p, x, cell(y), :] * elastic)
        return carry

    cells(final)
    d_store.wait()

    def order_out(i, carry):
        a, x = i // X, lax.rem(i, X)
        from_cells(lambda r: base[a, x, r, :], a, x)
        return carry

    lax.fori_loop(0, 3 * X, order_out, 0)
    o_store = pltpu.make_async_copy(nat.at[pl.ds(0, 3)], onew_hbm, osem.at[2])
    o_store.start()
    o_store.wait()


def solution(mesh):
    nx, ny = mesh.shape["gx"], mesh.shape["gy"]

    def step(conc, order):
        X, Y, Z = conc.shape
        S = Z // LANES
        f32 = jnp.float32
        N = nx * ny
        dma = pltpu.SemaphoreType.DMA
        anyspace = pl.BlockSpec(memory_space=pl.ANY)
        return pl.pallas_call(
            functools.partial(kernel, nx, ny, X, Y, S),
            out_shape=(jax.ShapeDtypeStruct(order.shape, f32), jax.ShapeDtypeStruct(conc.shape, f32),
                       jax.ShapeDtypeStruct(order.shape, f32)),
            in_specs=[anyspace] * 2,
            out_specs=[anyspace] * 3,
            scratch_shapes=[
                pltpu.VMEM((4, X, Y, Z), f32),
                pltpu.VMEM((2, 4, Y, Z), f32),
                pltpu.VMEM((4, X + 2, (Y + 2) * S, LANES), f32),
                pltpu.VMEM((3, 3, X + 2, (Y + 2) * S, LANES), f32),
                pltpu.VMEM((X + 2, (Y + 2) * S, LANES), f32),
                pltpu.VMEM((3, X, Y * S, LANES), f32),
                pltpu.VMEM((3, X + 2, (Y + 2) * S, LANES), f32),
                pltpu.VMEM((X, Y * S, LANES), f32),
                pltpu.VMEM((N, 1, LANES), f32),
                dma((2,)), dma((3,)), dma((6,)), dma((6,)),
                dma((3, 8)), dma((3, 8)), dma((4,)), dma((4,)), dma((N,)), dma((N,)),
            ],
            compiler_params=pltpu.CompilerParams(
                collective_id=0, has_side_effects=True, vmem_limit_bytes=48 << 20),
        )(conc, order)

    return jax.shard_map(
        step,
        mesh=mesh,
        in_specs=(P("gx", "gy", None), P(None, "gx", "gy", None)),
        out_specs=(P(None, "gx", "gy", None), P("gx", "gy", None), P(None, "gx", "gy", None)),
        check_vma=False,
    )
```

```python
import functools

import jax
import jax.numpy as jnp
from jax import lax
from jax.experimental import pallas as pl
from jax.experimental.pallas import tpu as pltpu
from jax.sharding import PartitionSpec as P

MESH = pl.DeviceIdType.MESH
LANES = 128
DIRS = [(dx, dy) for dx in (-1, 0, 1) for dy in (-1, 0, 1) if (dx, dy) != (0, 0)]
TIME_STEP = 0.02
DIAGONAL = 10.0


def kernel(nx, ny, X, Y, S, conc_hbm, order_hbm, disp_out, cnew_out, onew_out,
           nat, xh, ph, v, pot, base, od, oc, gat,
           lsem, a_send, a_recv, v_send, v_recv, g_send, g_recv):
    gx = lax.axis_index("gx")
    gy = lax.axis_index("gy")
    N = nx * ny
    me = gx * ny + gy
    lane = lax.broadcasted_iota(jnp.int32, (S, LANES), 1)
    sub = lax.broadcasted_iota(jnp.int32, (S, LANES), 0)
    last_lane = lane == LANES - 1
    first_lane = lane == 0
    z_end = jnp.logical_and(last_lane, sub == S - 1)
    z_start = jnp.logical_and(first_lane, sub == 0)
    zero = jnp.zeros((S, LANES), jnp.float32)

    loads = [
        pltpu.make_async_copy(conc_hbm, nat.at[0], lsem.at[0]),
        pltpu.make_async_copy(order_hbm, nat.at[pl.ds(1, 3)], lsem.at[1]),
    ]
    for item in loads:
        item.start()

    barrier = pltpu.get_barrier_semaphore()

    def greet(j, carry):
        t = lax.rem(me + j, N)
        pl.semaphore_signal(barrier, inc=1, device_id=(t // ny, lax.rem(t, ny)), device_id_type=MESH)
        return carry

    lax.fori_loop(1, N, greet, 0)

    def device(dx, dy):
        return (lax.rem(gx + dx + nx, nx), lax.rem(gy + dy + ny, ny))

    def remote(src, dst, send, recv, d):
        return pltpu.make_async_remote_copy(
            src_ref=src, dst_ref=dst, send_sem=send, recv_sem=recv,
            device_id=device(*d), device_id_type=MESH)

    def cell(y):
        return pl.ds(pl.multiple_of(y * S, S), S)

    def own(count, extent, step):
        if step == 0:
            return (pl.ds(1, extent), pl.ds(1, extent))
        return (pl.ds(1, 1), pl.ds(extent + 1, 1)) if step < 0 else (pl.ds(extent, 1), pl.ds(0, 1))

    def rows(part):
        return pl.ds(part.start * S, part.size * S)

    def to_cells(read, f, x):
        for y0 in range(0, Y, 8):
            for c in range(S):
                ph[f, x, pl.ds((2 + y0) * S + c, 8, stride=S), :] = read(y0, c)

    def relayout(i, carry):
        f, x = i // X, lax.rem(i, X)
        to_cells(lambda y0, c: nat[f, x, pl.ds(y0, 8), pl.ds(c * LANES, LANES)], f, x + 2)
        return carry

    for item in loads:
        item.wait()
    lax.fori_loop(0, 4 * X, relayout, 0)
    pl.semaphore_wait(barrier, N - 1)

    copies = []

    def send(src, dst, d):
        n = len(copies)
        copies.append(remote(src, dst, a_send.at[n], a_recv.at[n], d))
        copies[-1].start()

    def two(extent, step):
        if step < 0:
            return (2, extent + 2), (3, extent + 3), (2, extent + 2)
        return (extent + 1, 1), (extent, 0), (extent, 0)

    for dx, near, far, side in ((-1, 0, 1, 1), (1, X - 1, X - 2, 0)):
        send(conc_hbm.at[near], xh.at[side, 0], (dx, 0))
        send(order_hbm.at[:, near], xh.at[side, pl.ds(2, 3)], (dx, 0))
    for dx in (-1, 1):
        xn, xf, _ = two(X, dx)
        for dy in (-1, 1):
            yn, _, yb = two(Y, dy)
            send(ph.at[pl.ds(0, 3), xn[0], pl.ds(yb[0] * S, 2 * S)],
                 ph.at[pl.ds(0, 3), xn[1], pl.ds(yb[1] * S, 2 * S)], (dx, dy))
            send(ph.at[pl.ds(0, 2), xf[0], pl.ds(yn[0] * S, S)],
                 ph.at[pl.ds(0, 2), xf[1], pl.ds(yn[1] * S, S)], (dx, dy))
    for dx, near, far, side in ((-1, 0, 1, 1), (1, X - 1, X - 2, 0)):
        send(conc_hbm.at[far], xh.at[side, 1], (dx, 0))
        send(order_hbm.at[0, far], xh.at[side, 5], (dx, 0))
    for dy in (-1, 1):
        yn, _, yb = two(Y, dy)
        send(ph.at[pl.ds(0, 3), pl.ds(2, X), pl.ds(yb[0] * S, 2 * S)],
             ph.at[pl.ds(0, 3), pl.ds(2, X), pl.ds(yb[1] * S, 2 * S)], (0, dy))
        send(ph.at[3, pl.ds(2, X), pl.ds(yn[0] * S, S)],
             ph.at[3, pl.ds(2, X), pl.ds(yn[1] * S, S)], (0, dy))
    for item in copies:
        item.wait()

    def relayout_x(i, carry):
        for slot, f, far in ((0, 0, 0), (1, 0, 1), (2, 1, 0), (3, 2, 0), (4, 3, 0), (5, 1, 1)):
            row = (1 - far) + i * (X + 1 + 2 * far)
            to_cells(lambda y0, c: xh[i, slot, pl.ds(y0, 8), pl.ds(c * LANES, LANES)], f, row)
        return carry

    lax.fori_loop(0, 2, relayout_x, 0)

    def phase(f, x, y):
        return ph[f, x + 1, cell(y + 1), :]

    def up(a):
        r = pltpu.roll(a, LANES - 1, 1)
        return jnp.where(last_lane, pltpu.roll(r, S - 1, 0), r)

    def down(a):
        r = pltpu.roll(a, 1, 1)
        return jnp.where(first_lane, pltpu.roll(r, 1, 0), r)

    def up0(a):
        return jnp.where(z_end, 0.0, up(a))

    def down0(a):
        return jnp.where(z_start, 0.0, down(a))

    def cells(body, init=0, over=range(1, X + 1)):
        def outer(y, carry):
            for x in over:
                carry = body(x, y, carry)
            return carry
        return lax.fori_loop(1, Y + 1, outer, init)

    edge_rows = sorted({1, X})
    inner_rows = list(range(2, X))

    def eig(a, x, y):
        o = phase(1 + a, x, y)
        return phase(0, x, y) + o * o

    def rhs_at(x, y, comps):
        out = []
        for a in range(comps):
            if a == 0:
                r = -2.5 * (eig(0, x + 1, y) - eig(0, x - 1, y))
            elif a == 1:
                r = -2.5 * (eig(1, x, y + 1) - eig(1, x, y - 1))
            else:
                e = eig(2, x, y)
                r = -2.5 * (up(e) - down(e))
            v[0, a, x, cell(y), :] = r
            out.append(r)
        return out

    def rhs(x, y, carry):
        r0, r1, r2 = rhs_at(x, y, 3)
        return carry + (r0 * r0 + r1 * r1 + r2 * r2)

    def rhs_halo(x, y, carry):
        rhs_at(x, y, 3)
        return carry

    def y_halo(body):
        def outer(x, carry):
            for y in (0, Y + 1):
                body(x, y, 0)
            return carry
        lax.fori_loop(1, X + 1, outer, 0)

    acc0 = cells(rhs, zero)
    cells(rhs_halo, over=(0, X + 1))
    y_halo(rhs_halo)
    for x in (0, X + 1):
        for y in (0, Y + 1):
            rhs_at(x, y, 2)

    def valid(dx, dy):
        ok = None
        for g, n, d in ((gx, nx, dx), (gy, ny, dy)):
            if d:
                t = g > 0 if d < 0 else g < n - 1
                ok = t if ok is None else jnp.logical_and(ok, t)
        return ok

    def v_copy(k, n):
        dx, dy = DIRS[n]
        sx, tx = own(nx, X, dx)
        sy, ty = own(ny, Y, dy)
        comps = pl.ds(0, 2) if dx and dy else pl.ds(0, 1) if k == 2 and dx > 0 else pl.ds(0, 3)
        return remote(v.at[k, comps, sx, rows(sy)], v.at[k, comps, tx, rows(ty)],
                      v_send.at[k - 1, n], v_recv.at[k - 1, n], (dx, dy))

    def v_dirs(k):
        return [n for n in range(8) if not (k == 2 and DIRS[n][0] > 0 and DIRS[n][1])]

    def v_start(k, along_x):
        for n in sorted(v_dirs(k), key=lambda n: DIRS[n][1] != 0):
            if (DIRS[n][0] != 0) == along_x:
                @pl.when(valid(*DIRS[n]))
                def _(n=n):
                    v_copy(k, n).start()

    def v_wait(k):
        for n in v_dirs(k):
            dx, dy = DIRS[n]

            @pl.when(valid(dx, dy))
            def _():
                v_copy(k, n).wait_send()

            @pl.when(valid(-dx, -dy))
            def _():
                v_copy(k, n).wait_recv()

    def clear_x(row):
        def body(i, carry):
            for k in range(3):
                for a in range(3):
                    v[k, a, row, cell(i), :] = zero
            return carry
        lax.fori_loop(0, Y + 2, body, 0)

    def clear_y(col, low, high):
        for k in range(3):
            for a in range(3):
                for x in range(low, high):
                    v[k, a, x, cell(col), :] = zero

    for cond, row in ((gx == 0, 0), (gx == nx - 1, X + 1)):
        @pl.when(cond)
        def _(row=row):
            clear_x(row)
    for cond, col in ((gy == 0, 0), (gy == ny - 1, Y + 1)):
        @pl.when(cond)
        def _(col=col):
            clear_y(col, 0, X + 2)

    def laplace(read, x, y):
        c = read(x, y)
        s = read(x + 1, y) + read(x - 1, y) + read(x, y + 1) + read(x, y - 1)
        return s + up(c) + down(c) - 6.0 * c

    def potential(x, y, carry):
        c = phase(0, x, y)
        o = [phase(1 + p, x, y) for p in range(3)]
        total = o[0] * o[0] + o[1] * o[1] + o[2] * o[2]
        lap = laplace(functools.partial(phase, 0), x, y)
        pot[x, cell(y), :] = c * c * c - c - 0.5 * total - 0.5 * lap
        return carry

    def stencil(k, x, y, one_sided=False):
        def u(a, dx, dy):
            if one_sided and x + dx == 0:
                return zero
            value = v[k, a, x + dx, cell(y + dy), :]
            return 2.0 * value if one_sided and x + dx == X + 1 else value
        cross = []
        for a in (0, 1):
            cross.append(0.5 * (u(a, 1, 1) - u(a, 1, -1) - u(a, -1, 1) + u(a, -1, -1)))
        xp = [u(a, 1, 0) for a in range(3)]
        xm = [u(a, -1, 0) for a in range(3)]
        yp = [u(a, 0, 1) for a in range(3)]
        ym = [u(a, 0, -1) for a in range(3)]
        c = [u(a, 0, 0) for a in range(3)]
        g = 0.5 * (xp[2] - xm[2])
        h = 0.5 * (yp[2] - ym[2])
        w = 0.5 * ((xp[0] - xm[0]) + (yp[1] - ym[1]))
        i0 = 3.0 * (xp[0] + xm[0]) + (yp[0] + ym[0]) + cross[1] + up0(c[0] + g) + down0(c[0] - g)
        i1 = (xp[1] + xm[1]) + 3.0 * (yp[1] + ym[1]) + cross[0] + up0(c[1] + h) + down0(c[1] - h)
        c3 = 3.0 * c[2]
        i2 = (xp[2] + xm[2]) + (yp[2] + ym[2]) + up0(c3 + w) + down0(c3 - w)
        return c, [i0, i1, i2]

    scale = -1.0 / DIAGONAL

    def first(x, y, carry):
        d01, d11 = carry
        c, image = stencil(0, x, y)
        for a in range(3):
            new = scale * image[a]
            v[1, a, x, cell(y), :] = new
            d01 = d01 + c[a] * new
            d11 = d11 + new * new
        return d01, d11

    acc1 = cells(first, (zero, zero), edge_rows)
    v_start(1, True)
    acc1 = cells(first, acc1, inner_rows)
    v_start(1, False)
    cells(potential)
    cells(potential, over=(0, X + 1))
    y_halo(potential)

    def local(x, y, carry):
        c = phase(0, x, y)
        o = [phase(1 + p, x, y) for p in range(3)]
        q = [item * item for item in o]
        total = q[0] + q[1] + q[2]
        common = total - 1.0 - c
        for p in range(3):
            lap = laplace(functools.partial(phase, 1 + p), x, y)
            misfit = c + 2.5 * q[p] - 0.5 * total
            elastic = -5.0 * misfit
            drive = common * o[p] - 0.5 * lap - 2.0 * o[p] * elastic
            base[p, x - 1, cell(y - 1), :] = o[p] - TIME_STEP * drive
        return carry

    cells(local)

    def second(x, y, carry):
        d12, d22 = carry
        c, image = stencil(1, x, y)
        for a in range(3):
            new = (2.0 * scale) * image[a] - v[0, a, x, cell(y), :]
            v[2, a, x, cell(y), :] = new
            d12 = d12 + c[a] * new
            d22 = d22 + new * new
        return d12, d22

    v_wait(1)
    acc2 = cells(second, (zero, zero), edge_rows)
    v_start(2, True)
    acc2 = cells(second, acc2, inner_rows)
    v_start(2, False)

    def conc_step(x, y, carry):
        lap = laplace(lambda xx, yy: pot[xx, cell(yy), :], x, y)
        oc[x - 1, cell(y - 1), :] = phase(0, x, y) + TIME_STEP * lap
        return carry

    cells(conc_step)

    def from_cells(write, read, first):
        for y0 in range(0, Y, 8):
            for c in range(S):
                write(pl.ds(y0, 8), pl.ds(c * LANES, LANES), read(pl.ds((first + y0) * S + c, 8, stride=S)))

    def conc_out(x, carry):
        def write(r, l, value):
            cnew_out[x, r, l] = value
        from_cells(write, lambda r: oc[x, r, :], 0)
        return carry

    lax.fori_loop(0, X, conc_out, 0)

    def third(x, y, carry):
        c, image = stencil(2, x, y, True)
        return carry + (c[0] * image[0] + c[1] * image[1] + c[2] * image[2])

    v_wait(2)
    acc3 = scale * cells(third, zero)

    row_lane = lax.broadcasted_iota(jnp.int32, (1, LANES), 1)

    def reduce_all(a):
        return jnp.sum(jnp.sum(a, axis=0, keepdims=True), axis=1, keepdims=True)

    packed = jnp.zeros((1, LANES), jnp.float32)
    for n, item in enumerate((acc0, acc1[0], acc1[1], acc2[0], acc2[1], acc3)):
        packed = jnp.where(row_lane == n, reduce_all(item), packed)
    gat[me] = packed

    def g_copy(j, slot):
        t = lax.rem(me + j, N)
        return pltpu.make_async_remote_copy(
            src_ref=gat.at[slot], dst_ref=gat.at[slot], send_sem=g_send.at[j], recv_sem=g_recv.at[j],
            device_id=(t // ny, lax.rem(t, ny)), device_id_type=MESH)

    def g_start(j, carry):
        g_copy(j, me).start()
        return carry

    def g_wait(j, carry):
        g_copy(j, me).wait_send()
        g_copy(j, lax.rem(me + N - j, N)).wait_recv()
        return carry

    lax.fori_loop(1, N, g_start, 0)
    lax.fori_loop(1, N, g_wait, 0)
    tot = gat[0]
    for j in range(1, N):
        tot = tot + gat[j]
    m0, m1, d11, d12, d22, e = [
        jnp.sum(jnp.where(row_lane == n, tot, 0.0), axis=1, keepdims=True) for n in range(6)]

    g02 = 2.0 * d11 - m0
    G = [[m0, m1, g02], [m1, d11, d12], [g02, d12, d22]]
    h11 = 0.5 * (d12 + m1)
    h12 = 0.5 * (d22 + g02)
    H = [[m1, d11, d12], [d11, h11, h12], [d12, h12, e]]

    def form(mat, a, b):
        out = None
        for i in range(3):
            for j in range(3):
                if a[i] is not None and b[j] is not None:
                    term = a[i] * b[j] * mat[i][j]
                    out = term if out is None else out + term
        return out

    def plus(a, b):
        return b if a is None else (a if b is None else a + b)

    def times(s, a):
        return None if a is None else s * a

    A = [[DIAGONAL * (H[i][j] + G[i][j]) for j in range(3)] for i in range(3)]
    one = jnp.ones((1, 1), jnp.float32)
    xs, rs, ps = [None] * 3, [one, None, None], [one, None, None]
    rr = m0
    for it in range(3):
        alpha = rr / form(A, ps, ps)
        xs = [plus(xs[i], times(alpha, ps[i])) for i in range(3)]
        if it < 2:
            t = list(ps)
            t[1] = plus(t[1], ps[0])
            if ps[1] is not None:
                t[0] = plus(t[0], 0.5 * ps[1])
                t[2] = plus(t[2], 0.5 * ps[1])
            rs = [plus(rs[i], times(-DIAGONAL * alpha, t[i])) for i in range(3)]
            new = form(G, rs, rs)
            ps = [plus(rs[i], times(new / rr, ps[i])) for i in range(3)]
            rr = new
    co = [jnp.broadcast_to(item, (S, LANES)) for item in xs]

    def mix(a, x, y):
        return (co[0] * v[0, a, x, cell(y), :] + co[1] * v[1, a, x, cell(y), :]
                + co[2] * v[2, a, x, cell(y), :])

    def combine(x, y, carry):
        for a in range(3):
            od[a, x, cell(y), :] = mix(a, x, y)
        return carry

    cells(combine)

    def halo_x(y, carry):
        for x in (0, X + 1):
            od[0, x, cell(y), :] = mix(0, x, y)
        return carry

    lax.fori_loop(1, Y + 1, halo_x, 0)
    for x in range(1, X + 1):
        for y in (0, Y + 1):
            od[1, x, cell(y), :] = mix(1, x, y)

    def disp_store(i, carry):
        a, x = i // X, lax.rem(i, X)

        def write(r, l, value):
            disp_out[a, x, r, l] = value
        from_cells(write, lambda r: od[a, x + 1, r, :], 1)
        return carry

    lax.fori_loop(0, 3 * X, disp_store, 0)

    def final(x, y, carry):
        d2 = od[2, x, cell(y), :]
        strain = [
            0.5 * (od[0, x + 1, cell(y), :] - od[0, x - 1, cell(y), :]),
            0.5 * (od[1, x, cell(y + 1), :] - od[1, x, cell(y - 1), :]),
            0.5 * (up0(d2) - down0(d2)),
        ]
        for p in range(3):
            base[p, x - 1, cell(y - 1), :] = (
                base[p, x - 1, cell(y - 1), :]
                + (10.0 * TIME_STEP) * phase(1 + p, x, y) * strain[p])
        return carry

    cells(final)

    def order_store(i, carry):
        a, x = i // X, lax.rem(i, X)

        def write(r, l, value):
            onew_out[a, x, r, l] = value
        from_cells(write, lambda r: base[a, x, r, :], 0)
        return carry

    lax.fori_loop(0, 3 * X, order_store, 0)


def solution(mesh):
    nx, ny = mesh.shape["gx"], mesh.shape["gy"]

    def step(conc, order):
        X, Y, Z = conc.shape
        S = Z // LANES
        f32 = jnp.float32
        N = nx * ny
        dma = pltpu.SemaphoreType.DMA
        return pl.pallas_call(
            functools.partial(kernel, nx, ny, X, Y, S),
            out_shape=(jax.ShapeDtypeStruct(order.shape, f32), jax.ShapeDtypeStruct(conc.shape, f32),
                       jax.ShapeDtypeStruct(order.shape, f32)),
            in_specs=[pl.BlockSpec(memory_space=pltpu.HBM)] * 2,
            out_specs=[pl.BlockSpec(memory_space=pltpu.VMEM)] * 3,
            scratch_shapes=[
                pltpu.VMEM((4, X, Y, Z), f32),
                pltpu.VMEM((2, 6, Y, Z), f32),
                pltpu.VMEM((4, X + 4, (Y + 4) * S, LANES), f32),
                pltpu.VMEM((3, 3, X + 2, (Y + 2) * S, LANES), f32),
                pltpu.VMEM((X + 2, (Y + 2) * S, LANES), f32),
                pltpu.VMEM((3, X, Y * S, LANES), f32),
                pltpu.VMEM((3, X + 2, (Y + 2) * S, LANES), f32),
                pltpu.VMEM((X, Y * S, LANES), f32),
                pltpu.VMEM((N, 1, LANES), f32),
                dma((2,)), dma((20,)), dma((20,)), dma((2, 8)), dma((2, 8)), dma((N,)), dma((N,)),
            ],
            compiler_params=pltpu.CompilerParams(
                collective_id=0, has_side_effects=True, vmem_limit_bytes=48 << 20),
        )(conc, order)

    return jax.shard_map(
        step,
        mesh=mesh,
        in_specs=(P("gx", "gy", None), P(None, "gx", "gy", None)),
        out_specs=(P(None, "gx", "gy", None), P("gx", "gy", None), P(None, "gx", "gy", None)),
        check_vma=False,
    )
```

```python
import functools

import jax
import jax.numpy as jnp
from jax import lax
from jax.experimental import pallas as pl
from jax.experimental.pallas import tpu as pltpu
from jax.sharding import PartitionSpec as P

MESH = pl.DeviceIdType.MESH
LANES = 128
DIRS = [(dx, dy) for dx in (-1, 0, 1) for dy in (-1, 0, 1) if (dx, dy) != (0, 0)]
TIME_STEP = 0.02
DIAGONAL = 10.0


def kernel(nx, ny, X, Y, S, conc_hbm, order_hbm, disp_out, cnew_out, onew_out,
           nat, far_e, xh, ph, v, pot, base, od, oc, gat,
           lsem, a_send, a_recv, v_send, v_recv, g_send, g_recv):
    gx = lax.axis_index("gx")
    gy = lax.axis_index("gy")
    N = nx * ny
    me = gx * ny + gy
    lane = lax.broadcasted_iota(jnp.int32, (S, LANES), 1)
    sub = lax.broadcasted_iota(jnp.int32, (S, LANES), 0)
    last_lane = lane == LANES - 1
    first_lane = lane == 0
    z_end = jnp.logical_and(last_lane, sub == S - 1)
    z_start = jnp.logical_and(first_lane, sub == 0)
    zero = jnp.zeros((S, LANES), jnp.float32)

    loads = [
        pltpu.make_async_copy(conc_hbm, nat.at[0], lsem.at[0]),
        pltpu.make_async_copy(order_hbm, nat.at[pl.ds(1, 3)], lsem.at[1]),
    ]
    for item in loads:
        item.start()

    barrier = pltpu.get_barrier_semaphore()

    def greet(j, carry):
        t = lax.rem(me + j, N)
        pl.semaphore_signal(barrier, inc=1, device_id=(t // ny, lax.rem(t, ny)), device_id_type=MESH)
        return carry

    lax.fori_loop(1, N, greet, 0)

    def device(dx, dy):
        return (lax.rem(gx + dx + nx, nx), lax.rem(gy + dy + ny, ny))

    def remote(src, dst, send, recv, d):
        return pltpu.make_async_remote_copy(
            src_ref=src, dst_ref=dst, send_sem=send, recv_sem=recv,
            device_id=device(*d), device_id_type=MESH)

    def cell(y):
        return pl.ds(pl.multiple_of(y * S, S), S)

    def own(count, extent, step):
        if step == 0:
            return (pl.ds(1, extent), pl.ds(1, extent))
        return (pl.ds(1, 1), pl.ds(extent + 1, 1)) if step < 0 else (pl.ds(extent, 1), pl.ds(0, 1))

    def rows(part):
        return pl.ds(part.start * S, part.size * S)

    def to_cells(read, f, x):
        for y0 in range(0, Y, 8):
            for c in range(S):
                ph[f, x, pl.ds((2 + y0) * S + c, 8, stride=S), :] = read(y0, c)

    def spread(read, x):
        for y0 in range(0, Y, 8):
            for c in range(S):
                o = [read(1 + p, y0, c) for p in range(3)]
                conc = read(0, y0, c)
                for f, value in enumerate(o + [conc, conc + o[0] * o[0], conc + o[1] * o[1]]):
                    ph[f, x, pl.ds((2 + y0) * S + c, 8, stride=S), :] = value

    def relayout(x, carry):
        spread(lambda f, y0, c: nat[f, x, pl.ds(y0, 8), pl.ds(c * LANES, LANES)], x + 2)
        return carry

    for item in loads:
        item.wait()
    lax.fori_loop(0, X, relayout, 0)
    for side, far in ((1, 1), (0, X - 2)):
        far_e[side] = nat[0, far] + nat[1, far] * nat[1, far]
    pl.semaphore_wait(barrier, N - 1)

    copies = []

    def send(src, dst, d):
        n = len(copies)
        copies.append(remote(src, dst, a_send.at[n], a_recv.at[n], d))
        copies[-1].start()

    def two(extent, step):
        if step < 0:
            return (2, extent + 2), (3, extent + 3), (2, extent + 2)
        return (extent + 1, 1), (extent, 0), (extent, 0)

    for dx, near, side in ((-1, 0, 1), (1, X - 1, 0)):
        send(conc_hbm.at[near], xh.at[side, 0], (dx, 0))
        send(order_hbm.at[:, near], xh.at[side, pl.ds(1, 3)], (dx, 0))
        send(far_e.at[side], xh.at[side, 4], (dx, 0))
    for dx in (-1, 1):
        xn, xf, _ = two(X, dx)
        for dy in (-1, 1):
            yn, yf, _ = two(Y, dy)
            for fields, xx, yy in ((pl.ds(3, 3), xn, yn), (pl.ds(4, 1), xf, yn), (pl.ds(5, 1), xn, yf)):
                send(ph.at[fields, xx[0], pl.ds(yy[0] * S, S)],
                     ph.at[fields, xx[1], pl.ds(yy[1] * S, S)], (dx, dy))
    for dy in (-1, 1):
        yn, yf, _ = two(Y, dy)
        for fields, yy in ((pl.ds(0, 6), yn), (pl.ds(3, 3), yf)):
            send(ph.at[fields, pl.ds(2, X), pl.ds(yy[0] * S, S)],
                 ph.at[fields, pl.ds(2, X), pl.ds(yy[1] * S, S)], (0, dy))
    urgent = len(copies)
    for dx, far, side in ((-1, 1, 1), (1, X - 2, 0)):
        send(conc_hbm.at[far], xh.at[side, 5], (dx, 0))

    def up(a):
        r = pltpu.roll(a, LANES - 1, 1)
        return jnp.where(last_lane, pltpu.roll(r, S - 1, 0), r)

    def down(a):
        r = pltpu.roll(a, 1, 1)
        return jnp.where(first_lane, pltpu.roll(r, 1, 0), r)

    def up0(a):
        return jnp.where(z_end, 0.0, up(a))

    def down0(a):
        return jnp.where(z_start, 0.0, down(a))

    def cells(body, init=0, over=range(1, X + 1), low=1, high=Y + 1, unroll=2):
        def outer(y, carry):
            for x in over:
                carry = body(x, y, carry)
            return carry
        return lax.fori_loop(low, high, outer, init, unroll=unroll)

    edge_rows = sorted({1, X})
    inner_rows = list(range(2, X))

    def phase(f, x, y):
        return ph[f, x + 1, cell(y + 1), :]

    def rhs_at(x, y, comps):
        out = []
        for a in range(comps):
            if a == 0:
                r = -2.5 * (phase(4, x + 1, y) - phase(4, x - 1, y))
            elif a == 1:
                r = -2.5 * (phase(5, x, y + 1) - phase(5, x, y - 1))
            else:
                o = phase(2, x, y)
                e = phase(3, x, y) + o * o
                r = -2.5 * (up(e) - down(e))
            v[0, a, x, cell(y), :] = r
            out.append(r)
        return out

    def rhs(x, y, carry):
        out = rhs_at(x, y, 3)
        if 1 <= x <= X:
            carry = carry + (out[0] * out[0] + out[1] * out[1] + out[2] * out[2])
        return carry

    acc0 = cells(rhs, zero, inner_rows, 2, Y)
    for item in copies[:urgent]:
        item.wait()

    def relayout_x(i, carry):
        spread(lambda f, y0, c: xh[i, f, pl.ds(y0, 8), pl.ds(c * LANES, LANES)], 1 + i * (X + 1))
        to_cells(lambda y0, c: xh[i, 4, pl.ds(y0, 8), pl.ds(c * LANES, LANES)], 4, i * (X + 3))
        return carry

    lax.fori_loop(0, 2, relayout_x, 0)
    acc0 = cells(rhs, acc0, [0] + edge_rows + [X + 1])
    for x in inner_rows:
        for y in (1, Y):
            acc0 = rhs(x, y, acc0)
    for x in range(0, X + 2):
        for y in (0, Y + 1):
            rhs_at(x, y, 3 if 1 <= x <= X else 2)

    def y_halo(body):
        def outer(x, carry):
            for y in (0, Y + 1):
                body(x, y, 0)
            return carry
        lax.fori_loop(1, X + 1, outer, 0, unroll=2)

    def valid(dx, dy):
        ok = None
        for g, n, d in ((gx, nx, dx), (gy, ny, dy)):
            if d:
                t = g > 0 if d < 0 else g < n - 1
                ok = t if ok is None else jnp.logical_and(ok, t)
        return ok

    def v_copy(k, n):
        dx, dy = DIRS[n]
        sx, tx = own(nx, X, dx)
        sy, ty = own(ny, Y, dy)
        comps = pl.ds(0, 2) if dx and dy else pl.ds(0, 1) if k == 2 and dx > 0 else pl.ds(0, 3)
        return remote(v.at[k, comps, sx, rows(sy)], v.at[k, comps, tx, rows(ty)],
                      v_send.at[k - 1, n], v_recv.at[k - 1, n], (dx, dy))

    def v_dirs(k):
        return [n for n in range(8) if not (k == 2 and DIRS[n][0] > 0 and DIRS[n][1])]

    def v_start(k, along_x):
        for n in sorted(v_dirs(k), key=lambda n: DIRS[n][1] != 0):
            if (DIRS[n][0] != 0) == along_x:
                @pl.when(valid(*DIRS[n]))
                def _(n=n):
                    v_copy(k, n).start()

    def v_wait(k):
        for n in v_dirs(k):
            dx, dy = DIRS[n]

            @pl.when(valid(dx, dy))
            def _():
                v_copy(k, n).wait_send()

            @pl.when(valid(-dx, -dy))
            def _():
                v_copy(k, n).wait_recv()

    def clear_x(row):
        def body(i, carry):
            for k in range(3):
                for a in range(3):
                    v[k, a, row, cell(i), :] = zero
            return carry
        lax.fori_loop(0, Y + 2, body, 0)

    def clear_y(col, low, high):
        for k in range(3):
            for a in range(3):
                for x in range(low, high):
                    v[k, a, x, cell(col), :] = zero

    for cond, row in ((gx == 0, 0), (gx == nx - 1, X + 1)):
        @pl.when(cond)
        def _(row=row):
            clear_x(row)
    for cond, col in ((gy == 0, 0), (gy == ny - 1, Y + 1)):
        @pl.when(cond)
        def _(col=col):
            clear_y(col, 0, X + 2)

    def laplace(read, x, y):
        c = read(x, y)
        s = read(x + 1, y) + read(x - 1, y) + read(x, y + 1) + read(x, y - 1)
        return s + up(c) + down(c) - 6.0 * c

    def potential(x, y, carry):
        c = phase(3, x, y)
        o = [phase(p, x, y) for p in range(3)]
        total = o[0] * o[0] + o[1] * o[1] + o[2] * o[2]
        lap = laplace(functools.partial(phase, 3), x, y)
        pot[x, cell(y), :] = c * c * c - c - 0.5 * total - 0.5 * lap
        return carry

    def stencil(k, x, y, one_sided=False):
        def u(a, dx, dy):
            if one_sided and x + dx == 0:
                return zero
            value = v[k, a, x + dx, cell(y + dy), :]
            return 2.0 * value if one_sided and x + dx == X + 1 else value
        cross = []
        for a in (0, 1):
            cross.append(0.5 * (u(a, 1, 1) - u(a, 1, -1) - u(a, -1, 1) + u(a, -1, -1)))
        xp = [u(a, 1, 0) for a in range(3)]
        xm = [u(a, -1, 0) for a in range(3)]
        yp = [u(a, 0, 1) for a in range(3)]
        ym = [u(a, 0, -1) for a in range(3)]
        c = [u(a, 0, 0) for a in range(3)]
        g = 0.5 * (xp[2] - xm[2])
        h = 0.5 * (yp[2] - ym[2])
        w = 0.5 * ((xp[0] - xm[0]) + (yp[1] - ym[1]))
        i0 = 3.0 * (xp[0] + xm[0]) + (yp[0] + ym[0]) + cross[1] + up0(c[0] + g) + down0(c[0] - g)
        i1 = (xp[1] + xm[1]) + 3.0 * (yp[1] + ym[1]) + cross[0] + up0(c[1] + h) + down0(c[1] - h)
        c3 = 3.0 * c[2]
        i2 = (xp[2] + xm[2]) + (yp[2] + ym[2]) + up0(c3 + w) + down0(c3 - w)
        return c, [i0, i1, i2]

    scale = -1.0 / DIAGONAL

    def first(x, y, carry):
        d01, d11 = carry
        c, image = stencil(0, x, y)
        for a in range(3):
            new = scale * image[a]
            v[1, a, x, cell(y), :] = new
            d01 = d01 + c[a] * new
            d11 = d11 + new * new
        return d01, d11

    acc1 = cells(first, (zero, zero), edge_rows)
    v_start(1, True)
    acc1 = cells(first, acc1, inner_rows)
    v_start(1, False)
    for item in copies[urgent:]:
        item.wait()
    for side in range(2):
        to_cells(lambda y0, c: xh[side, 5, pl.ds(y0, 8), pl.ds(c * LANES, LANES)], 3, side * (X + 3))
    cells(potential, over=range(0, X + 2))
    y_halo(potential)

    def local(x, y, carry):
        c = phase(3, x, y)
        o = [phase(p, x, y) for p in range(3)]
        q = [item * item for item in o]
        total = q[0] + q[1] + q[2]
        common = total - 1.0 - c
        for p in range(3):
            lap = laplace(functools.partial(phase, p), x, y)
            misfit = c + 2.5 * q[p] - 0.5 * total
            elastic = -5.0 * misfit
            drive = common * o[p] - 0.5 * lap - 2.0 * o[p] * elastic
            base[p, x - 1, cell(y - 1), :] = o[p] - TIME_STEP * drive
        return carry

    cells(local)

    def second(x, y, carry):
        d12, d22 = carry
        c, image = stencil(1, x, y)
        for a in range(3):
            new = (2.0 * scale) * image[a] - v[0, a, x, cell(y), :]
            v[2, a, x, cell(y), :] = new
            d12 = d12 + c[a] * new
            d22 = d22 + new * new
        return d12, d22

    v_wait(1)
    acc2 = cells(second, (zero, zero), edge_rows)
    v_start(2, True)
    acc2 = cells(second, acc2, inner_rows)
    v_start(2, False)

    def conc_step(x, y, carry):
        lap = laplace(lambda xx, yy: pot[xx, cell(yy), :], x, y)
        oc[x - 1, cell(y - 1), :] = phase(3, x, y) + TIME_STEP * lap
        return carry

    cells(conc_step)

    def from_cells(write, read, first):
        for y0 in range(0, Y, 8):
            for c in range(S):
                write(pl.ds(y0, 8), pl.ds(c * LANES, LANES), read(pl.ds((first + y0) * S + c, 8, stride=S)))

    def conc_out(x, carry):
        def write(r, l, value):
            cnew_out[x, r, l] = value
        from_cells(write, lambda r: oc[x, r, :], 0)
        return carry

    lax.fori_loop(0, X, conc_out, 0)

    def third(x, y, carry):
        c, image = stencil(2, x, y, True)
        return carry + (c[0] * image[0] + c[1] * image[1] + c[2] * image[2])

    v_wait(2)
    acc3 = scale * cells(third, zero)

    row_lane = lax.broadcasted_iota(jnp.int32, (1, LANES), 1)

    def reduce_all(a):
        return jnp.sum(jnp.sum(a, axis=0, keepdims=True), axis=1, keepdims=True)

    packed = jnp.zeros((1, LANES), jnp.float32)
    for n, item in enumerate((acc0, acc1[0], acc1[1], acc2[0], acc2[1], acc3)):
        packed = jnp.where(row_lane == n, reduce_all(item), packed)
    gat[me] = packed

    def g_copy(j, slot):
        t = lax.rem(me + j, N)
        return pltpu.make_async_remote_copy(
            src_ref=gat.at[slot], dst_ref=gat.at[slot], send_sem=g_send.at[j], recv_sem=g_recv.at[j],
            device_id=(t // ny, lax.rem(t, ny)), device_id_type=MESH)

    def g_start(j, carry):
        g_copy(j, me).start()
        return carry

    def g_wait(j, carry):
        g_copy(j, me).wait_send()
        g_copy(j, lax.rem(me + N - j, N)).wait_recv()
        return carry

    lax.fori_loop(1, N, g_start, 0)
    lax.fori_loop(1, N, g_wait, 0)
    tot = gat[0]
    for j in range(1, N):
        tot = tot + gat[j]
    m0, m1, d11, d12, d22, e = [
        jnp.sum(jnp.where(row_lane == n, tot, 0.0), axis=1, keepdims=True) for n in range(6)]

    g02 = 2.0 * d11 - m0
    G = [[m0, m1, g02], [m1, d11, d12], [g02, d12, d22]]
    h11 = 0.5 * (d12 + m1)
    h12 = 0.5 * (d22 + g02)
    H = [[m1, d11, d12], [d11, h11, h12], [d12, h12, e]]

    def form(mat, a, b):
        out = None
        for i in range(3):
            for j in range(3):
                if a[i] is not None and b[j] is not None:
                    term = a[i] * b[j] * mat[i][j]
                    out = term if out is None else out + term
        return out

    def plus(a, b):
        return b if a is None else (a if b is None else a + b)

    def times(s, a):
        return None if a is None else s * a

    A = [[DIAGONAL * (H[i][j] + G[i][j]) for j in range(3)] for i in range(3)]
    one = jnp.ones((1, 1), jnp.float32)
    xs, rs, ps = [None] * 3, [one, None, None], [one, None, None]
    rr = m0
    for it in range(3):
        alpha = rr / form(A, ps, ps)
        xs = [plus(xs[i], times(alpha, ps[i])) for i in range(3)]
        if it < 2:
            t = list(ps)
            t[1] = plus(t[1], ps[0])
            if ps[1] is not None:
                t[0] = plus(t[0], 0.5 * ps[1])
                t[2] = plus(t[2], 0.5 * ps[1])
            rs = [plus(rs[i], times(-DIAGONAL * alpha, t[i])) for i in range(3)]
            new = form(G, rs, rs)
            ps = [plus(rs[i], times(new / rr, ps[i])) for i in range(3)]
            rr = new
    co = [jnp.broadcast_to(item, (S, LANES)) for item in xs]

    def mix(a, x, y):
        return (co[0] * v[0, a, x, cell(y), :] + co[1] * v[1, a, x, cell(y), :]
                + co[2] * v[2, a, x, cell(y), :])

    def combine(x, y, carry):
        for a in range(3):
            od[a, x, cell(y), :] = mix(a, x, y)
        return carry

    cells(combine)

    def halo_x(y, carry):
        for x in (0, X + 1):
            od[0, x, cell(y), :] = mix(0, x, y)
        return carry

    lax.fori_loop(1, Y + 1, halo_x, 0)
    for x in range(1, X + 1):
        for y in (0, Y + 1):
            od[1, x, cell(y), :] = mix(1, x, y)

    def disp_store(i, carry):
        a, x = i // X, lax.rem(i, X)

        def write(r, l, value):
            disp_out[a, x, r, l] = value
        from_cells(write, lambda r: od[a, x + 1, r, :], 1)
        return carry

    lax.fori_loop(0, 3 * X, disp_store, 0)

    def final(x, y, carry):
        d2 = od[2, x, cell(y), :]
        strain = [
            0.5 * (od[0, x + 1, cell(y), :] - od[0, x - 1, cell(y), :]),
            0.5 * (od[1, x, cell(y + 1), :] - od[1, x, cell(y - 1), :]),
            0.5 * (up0(d2) - down0(d2)),
        ]
        for p in range(3):
            base[p, x - 1, cell(y - 1), :] = (
                base[p, x - 1, cell(y - 1), :]
                + (10.0 * TIME_STEP) * phase(p, x, y) * strain[p])
        return carry

    cells(final)

    def order_store(i, carry):
        a, x = i // X, lax.rem(i, X)

        def write(r, l, value):
            onew_out[a, x, r, l] = value
        from_cells(write, lambda r: base[a, x, r, :], 0)
        return carry

    lax.fori_loop(0, 3 * X, order_store, 0)


def solution(mesh):
    nx, ny = mesh.shape["gx"], mesh.shape["gy"]

    def step(conc, order):
        X, Y, Z = conc.shape
        S = Z // LANES
        f32 = jnp.float32
        N = nx * ny
        dma = pltpu.SemaphoreType.DMA
        return pl.pallas_call(
            functools.partial(kernel, nx, ny, X, Y, S),
            out_shape=(jax.ShapeDtypeStruct(order.shape, f32), jax.ShapeDtypeStruct(conc.shape, f32),
                       jax.ShapeDtypeStruct(order.shape, f32)),
            in_specs=[pl.BlockSpec(memory_space=pltpu.HBM)] * 2,
            out_specs=[pl.BlockSpec(memory_space=pltpu.VMEM)] * 3,
            scratch_shapes=[
                pltpu.VMEM((4, X, Y, Z), f32),
                pltpu.VMEM((2, Y, Z), f32),
                pltpu.VMEM((2, 6, Y, Z), f32),
                pltpu.VMEM((6, X + 4, (Y + 4) * S, LANES), f32),
                pltpu.VMEM((3, 3, X + 2, (Y + 2) * S, LANES), f32),
                pltpu.VMEM((X + 2, (Y + 2) * S, LANES), f32),
                pltpu.VMEM((3, X, Y * S, LANES), f32),
                pltpu.VMEM((3, X + 2, (Y + 2) * S, LANES), f32),
                pltpu.VMEM((X, Y * S, LANES), f32),
                pltpu.VMEM((N, 1, LANES), f32),
                dma((2,)), dma((24,)), dma((24,)), dma((2, 8)), dma((2, 8)), dma((N,)), dma((N,)),
            ],
            compiler_params=pltpu.CompilerParams(
                collective_id=0, has_side_effects=True, vmem_limit_bytes=48 << 20),
        )(conc, order)

    return jax.shard_map(
        step,
        mesh=mesh,
        in_specs=(P("gx", "gy", None), P(None, "gx", "gy", None)),
        out_specs=(P(None, "gx", "gy", None), P("gx", "gy", None), P(None, "gx", "gy", None)),
        check_vma=False,
    )
```
